256 devices in a mesh: rows: 128 (over x, y_hi, z, core), cols: 2 (over y_lo).
Axes of the slice: x: 4, y: 4 (y_hi: 2, y_lo: 2; y = y_hi * 2 + y_lo), z: 8, core: 2. Of those that a mesh axis runs over, the one named last changes fastest.
Arguments:
- ancestor: bfloat16 [24576, 24576], P('rows', 'cols'), may hold values from -6 to 6
- panel_below: bfloat16 [2048, 512], P('rows'), may hold values from -0.0625 to 0.0625
- panel_beside: bfloat16 [2048, 512], P('rows'), may hold values from -0.0625 to 0.0625
- inverse_lower: bfloat16 [512, 512], replicated, may hold values from -3 to 3
- inverse_upper: bfloat16 [512, 512], replicated, may hold values from -3 to 3
- list_below: int32 [16], replicated, may hold values from 0 to 191, as said below
- list_beside: int32 [16], replicated, may hold values from 0 to 191, as said below
- second_below: bfloat16 [2048, 512], P('rows'), may hold values from -0.0625 to 0.0625
- second_beside: bfloat16 [2048, 512], P('rows'), may hold values from -0.0625 to 0.0625
- linked_below: bfloat16 [512, 512], replicated, may hold values from -0.0625 to 0.0625
- linked_beside: bfloat16 [512, 512], replicated, may hold values from -0.0625 to 0.0625
- second_lower: bfloat16 [512, 512], replicated, may hold values from -3 to 3
- second_upper: bfloat16 [512, 512], replicated, may hold values from -3 to 3
- blocks_below: int32 [16], replicated, may hold values from 0 to 191, as said below
- blocks_beside: int32 [16], replicated, may hold values from 0 to 191, as said below
Outputs:
- new_lower: bfloat16 [24576, 512], P('rows', 'cols')
- new_upper: bfloat16 [24576, 512], P(('cols', 'rows'))
- new_diagonal: bfloat16 [512, 512], P(None, 'cols')
- next_lower: bfloat16 [24576, 512], P('rows', 'cols')
- next_upper: bfloat16 [24576, 512], P(('cols', 'rows'))
- next_link: bfloat16 [512, 512], replicated
- next_diagonal: bfloat16 [512, 512], P(None, 'cols')
The draws below stay inside these ranges and needn't reach their ends.
Inputs may be any that keep to these rules, and one draw needn't show every extreme that they name: `list_below`: 16 distinct block numbers in ascending order; block 0 and block 191 are always listed. `list_beside`: 16 distinct block numbers in ascending order; block 0 and block 191 are always listed. `blocks_below`: 16 distinct block numbers in ascending order; block 0 and block 191 are always listed. `blocks_beside`: 16 distinct block numbers in ascending order; block 0 and block 191 are always listed.
All inputs are finite; a program needn't handle non-finite values.
Results may differ from the reference program's by a relative error of at most 0.0077.
Values may be sent and summed in bfloat16 or wider, within the bound.
A program may use at most 128 MiB of HBM per device.

```python
import jax
import jax.numpy as jnp

M = 24576
W = 512
BLK = 128
R = 16
P_SIZE = 2048


def pick_blocks(key, salt_value):
    folded = jax.random.fold_in(key, salt_value)
    shuffled = jax.random.permutation(folded, M // BLK - 2) + 1
    chosen = shuffled[:R - 2].astype(jnp.int32)
    listed = jnp.concatenate([jnp.zeros((1,), jnp.int32), chosen, jnp.full((1,), M // BLK - 1, jnp.int32)])
    return jnp.sort(listed)


def draw_list_below(key, part):
    return pick_blocks(key, 11)


def draw_list_beside(key, part):
    return pick_blocks(key, 23)


def draw_blocks_below(key, part):
    return pick_blocks(key, 37)


def draw_blocks_beside(key, part):
    return pick_blocks(key, 41)


def level_of(key, shape, split, low, top_value):
    loudness = 1.0
    for axis_at, shards_of in split:
        draws = jax.random.uniform(jax.random.fold_in(jax.random.fold_in(key, 6), axis_at), (shards_of,), jnp.float32, low / len(split), top_value / len(split))
        loudness = loudness * jnp.repeat(jnp.exp(draws), shape[axis_at] // shards_of).reshape((-1,) + (1,) * (len(shape) - 1 - axis_at))
    return loudness


def normal_values(own_key, dims, deviation, limit, cuts=(), dtype=jnp.bfloat16):
    drawn = deviation * jax.random.normal(own_key, dims, jnp.float32)
    if cuts:
        drawn = drawn * level_of(own_key, dims, cuts, -0.22, 0.18)
    return jnp.clip(drawn, -limit, limit).astype(dtype)


def setup_inputs(seed: int = 0) -> dict:
    keys = jax.random.split(jax.random.key(seed), 16)
    return {
        "ancestor": normal_values(keys[0], (M, M), 1.0, 6.0, ((0, 128), (1, 2))),
        "panel_below": normal_values(keys[1], (P_SIZE, W), ((R * BLK) ** -0.5 * W ** -0.25), 0.0625, ((0, 128),)),
        "panel_beside": normal_values(keys[2], (P_SIZE, W), ((R * BLK) ** -0.5 * W ** -0.25), 0.0625, ((0, 128),)),
        "inverse_lower": normal_values(keys[3], (W, W), (W ** -0.25), 3.0),
        "inverse_upper": normal_values(keys[4], (W, W), (W ** -0.25), 3.0),
        "list_below": draw_list_below(jax.random.fold_in(keys[15], 71), 0),
        "list_beside": draw_list_beside(jax.random.fold_in(keys[15], 71), 0),
        "second_below": normal_values(keys[7], (P_SIZE, W), ((R * BLK) ** -0.5 * W ** -0.25), 0.0625, ((0, 128),)),
        "second_beside": normal_values(keys[8], (P_SIZE, W), ((R * BLK) ** -0.5 * W ** -0.25), 0.0625, ((0, 128),)),
        "linked_below": normal_values(keys[9], (W, W), ((R * BLK) ** -0.5 * W ** -0.25), 0.0625),
        "linked_beside": normal_values(keys[10], (W, W), ((R * BLK) ** -0.5 * W ** -0.25), 0.0625),
        "second_lower": normal_values(keys[11], (W, W), (W ** -0.25), 3.0),
        "second_upper": normal_values(keys[12], (W, W), (W ** -0.25), 3.0),
        "blocks_below": draw_blocks_below(jax.random.fold_in(keys[15], 71), 0),
        "blocks_beside": draw_blocks_beside(jax.random.fold_in(keys[15], 71), 0),
    }


def normalise(panel, inverse):
    return jnp.dot(panel, inverse, preferred_element_type=jnp.float32).astype(jnp.bfloat16)


def normalise_by_rows(panel, inverse):
    return jnp.dot(panel, inverse.T, preferred_element_type=jnp.float32).astype(jnp.bfloat16)


def rows_from(matrix, blocks):
    shaped = matrix.reshape(M // BLK, BLK, matrix.shape[1])
    return jnp.take(shaped, blocks, axis=0).reshape(R * BLK, matrix.shape[1])


def columns_of(matrix, blocks):
    shaped = matrix.reshape(matrix.shape[0], M // BLK, BLK)
    return jnp.take(shaped, blocks, axis=1).reshape(matrix.shape[0], R * BLK)


def reference(ancestor, panel_below, panel_beside, inverse_lower, inverse_upper, list_below, list_beside, second_below, second_beside, linked_below, linked_beside, second_lower, second_upper, blocks_below, blocks_beside):
    unit_below = normalise(panel_below, inverse_lower)
    unit_beside = normalise_by_rows(panel_beside, inverse_upper)
    new_lower = (-jnp.dot(columns_of(ancestor, list_below), unit_below, preferred_element_type=jnp.float32)).astype(jnp.bfloat16)
    new_upper = (-jnp.dot(rows_from(ancestor, list_beside).T, unit_beside, preferred_element_type=jnp.float32)).astype(jnp.bfloat16)
    new_diagonal = (jnp.dot(inverse_upper, inverse_lower, preferred_element_type=jnp.float32)
                    - jnp.dot(unit_beside.T, rows_from(new_lower, list_beside), preferred_element_type=jnp.float32)).astype(jnp.bfloat16)
    below_next = normalise(second_below, second_lower)
    link_below = normalise(linked_below, second_lower)
    beside_next = normalise_by_rows(second_beside, second_upper)
    link_beside = normalise_by_rows(linked_beside, second_upper)
    next_lower = (-(jnp.dot(columns_of(ancestor, blocks_below), below_next, preferred_element_type=jnp.float32)
                    + jnp.dot(new_lower, link_below, preferred_element_type=jnp.float32))).astype(jnp.bfloat16)
    next_link = (-(jnp.dot(rows_from(new_upper, blocks_below).T, below_next, preferred_element_type=jnp.float32)
                   + jnp.dot(new_diagonal, link_below, preferred_element_type=jnp.float32))).astype(jnp.bfloat16)
    next_upper = (-(jnp.dot(rows_from(ancestor, blocks_beside).T, beside_next, preferred_element_type=jnp.float32)
                    + jnp.dot(new_upper, link_beside, preferred_element_type=jnp.float32))).astype(jnp.bfloat16)
    next_diagonal = (jnp.dot(second_upper, second_lower, preferred_element_type=jnp.float32)
                     - jnp.dot(beside_next.T, rows_from(next_lower, blocks_beside), preferred_element_type=jnp.float32)
                     - jnp.dot(link_beside.T, next_link, preferred_element_type=jnp.float32)).astype(jnp.bfloat16)
    return new_lower, new_upper, new_diagonal, next_lower, next_upper, next_link, next_diagonal
```

```python
import jax
import jax.numpy as jnp
from jax import lax
from jax.experimental import pallas as pl
from jax.experimental.pallas import tpu as pltpu
from jax.sharding import PartitionSpec as P

MESH = pl.DeviceIdType.MESH
F32 = jnp.float32
BF16 = jnp.bfloat16
NX, NY, NZ, NK = 4, 2, 8, 2
NXY = NX * NY
NQ = NXY * NK
ND = NQ * 2
BLK = 128
W = 512
HALF = 256
R = 16
ROWS = 192
COLS = 12288
STRIP = COLS // NQ
OWN = 96


def dot(a, b):
    return jnp.dot(a, b, preferred_element_type=F32)


def dot_rows(a, b):
    return lax.dot_general(a, b, (((0,), (0,)), ((), ())), preferred_element_type=F32)


def dot_cols(a, b):
    return lax.dot_general(a, b, (((1,), (1,)), ((), ())), preferred_element_type=F32)


def kept(block, keep):
    scale = jnp.full((1, block.shape[1]), keep.astype(jnp.int32).astype(F32), F32).astype(BF16)
    return block * scale


def each(n, body):
    def step(i, carry):
        body(i)
        return carry

    lax.fori_loop(0, n, step, 0)


def kernel(
    anc, p_below, p_beside, inv_l, inv_u, s_below, s_beside, lk_below, lk_beside, sec_l, sec_u,
    list_below, list_beside, blocks_below, blocks_beside,
    o_lower, o_upper, o_diag, o_nlower, o_nupper, o_link, o_ndiag,
    tile, strip, unit, pick_l, pick_u, onto, prod, low_s, low_r, sums_s, sums_r, zsum, fin, up_s, up_r,
    link_b, link_s, base1, base2,
    loc_sem, gy_s, gy_r, gx_s, gx_r, zr_s, zr_r, zl_s, zl_r, gc_s, gc_r,
    aa_s, aa_r, lw_s, lw_r, sm_s, sm_r, zs_s, zs_r, fn_s, fn_r, up_ss, up_rs,
):
    row = lax.axis_index("rows")
    col = lax.axis_index("cols")
    core = lax.rem(row, NK)
    z = lax.rem(lax.div(row, NK), NZ)
    xy = lax.div(row, NK * NZ)
    x = lax.div(xy, NY)
    yh = lax.rem(xy, NY)
    q = xy * NK + core
    d = q * 2 + col

    def row_of(xy_, z_, core_):
        return (xy_ * NZ + z_) * NK + core_

    def copy(src, dst, s, r, to_row, to_col):
        return pltpu.make_async_remote_copy(
            src_ref=src, dst_ref=dst, send_sem=s, recv_sem=r,
            device_id=(to_row, to_col), device_id_type=MESH,
        )

    def strip_cols(q_):
        return pl.ds(pl.multiple_of(q_ * STRIP, BLK), STRIP)

    own_half = pl.ds(pl.multiple_of(col * HALF, BLK), HALF)
    other_half = pl.ds(pl.multiple_of((1 - col) * HALF, BLK), HALF)

    def load_block(j):
        pltpu.make_async_copy(
            anc.at[:, :, pl.ds(pl.multiple_of(j * BLK, BLK), BLK)], tile.at[j], loc_sem.at[0]
        ).start()

    each(COLS // BLK, load_block)
    load_strip = pltpu.make_async_copy(
        anc.at[:, :, strip_cols(q)], strip.at[pl.ds(q * 3, 3)], loc_sem.at[1]
    )
    load_strip.start()

    unit[0, xy, z, core] = dot(p_below[...], inv_l[...]).astype(BF16)
    unit[1, xy, z, core] = dot(s_below[...], sec_l[...]).astype(BF16)
    unit[2, xy, z, core] = dot_cols(p_beside[...], inv_u[...]).astype(BF16)
    unit[3, xy, z, core] = dot_cols(s_beside[...], sec_u[...]).astype(BF16)

    barrier = pltpu.get_barrier_semaphore()

    def greet_plane(i):
        peer = lax.rem(d + 1 + i, ND)
        pq = lax.div(peer, 2)
        pl.semaphore_signal(
            barrier, inc=1,
            device_id=(row_of(lax.div(pq, NK), z, lax.rem(pq, NK)), lax.rem(peer, 2)),
            device_id_type=MESH,
        )

    def greet_line(i):
        peer = lax.rem(z + 1 + lax.div(i, NK), NZ)
        pl.semaphore_signal(
            barrier, inc=1, device_id=(row_of(xy, peer, lax.rem(i, NK)), col), device_id_type=MESH
        )

    each(ND - 1, greet_plane)
    each((NZ - 1) * NK, greet_line)
    pl.semaphore_wait(barrier, ND - 1 + (NZ - 1) * NK)

    nxy = x * NY + (1 - yh)
    mine = unit.at[:, xy, z, core]
    y_out = copy(mine, mine, gy_s.at[0], gy_r.at[0], row_of(nxy, z, core), 1 - col)
    y_out.start()
    theirs = unit.at[:, nxy, z, core]
    copy(theirs, theirs, gy_s.at[0], gy_r.at[0], row_of(nxy, z, core), 1 - col).wait_recv()

    def x_copy(i, holder, to):
        part = unit.at[:, pl.ds(holder * NY, NY), z, core]
        return copy(part, part, gx_s.at[i - 1], gx_r.at[i - 1], row_of(to * NY + yh, z, core), col)

    for i in (1, 3, 2):
        x_copy(i, x, lax.rem(x + i, NX)).start()

    def aa_copy(i, src_q, to_q):
        return copy(
            anc.at[:, :, strip_cols(to_q)],
            strip.at[pl.ds(src_q * 3, 3)],
            aa_s.at[i], aa_r.at[i],
            row_of(lax.div(to_q, NK), z, lax.rem(to_q, NK)), col,
        )

    each(NQ - 1, lambda i: aa_copy(i, q, lax.rem(q + 1 + i, NQ)).start())

    for i in (1, 3, 2):
        frm = lax.rem(x + NX - i, NX)
        x_copy(i, frm, frm).wait_recv()

    right, left = lax.rem(z + 1, NZ), lax.rem(z + NZ - 1, NZ)

    def chunk(zz, lo, n):
        return unit.at[pl.ds(lo, n), :, zz, core]

    def to_right(t, zz):
        part = chunk(zz, 0, 4 if t < 3 else 2)
        return copy(part, part, zr_s.at[t], zr_r.at[t], row_of(xy, right, core), col)

    def to_left(t, zz):
        part = chunk(zz, 0 if t < 3 else 2, 4 if t < 3 else 2)
        return copy(part, part, zl_s.at[t], zl_r.at[t], row_of(xy, left, core), col)

    def to_core(o, k):
        part = unit.at[:, :, lax.rem(z + o, NZ), k]
        return copy(part, part, gc_s.at[o], gc_r.at[o], row_of(xy, z, 1 - core), col)

    def at(o):
        return lax.rem(z + NZ + o, NZ)

    to_right(0, z).start()
    to_left(0, z).start()
    to_core(0, core).start()

    def small(i):
        part = pl.ds(pl.multiple_of(i * BLK, BLK), BLK)
        link_b[part, :] = dot(lk_below[part, :], sec_l[...]).astype(BF16)
        link_s[part, :] = dot_cols(lk_beside[part, :], sec_u[...]).astype(BF16)
        base2[part, :] = dot(sec_u[part, :], sec_l[:, own_half])

    each(4, small)
    base1[...] = dot(inv_u[pl.ds(pl.multiple_of(d * 16, 16), 16), :], inv_l[...])

    for t in range(4):
        to_right(t, at(-1 - t)).wait_recv()
        if t < 3:
            to_right(t + 1, at(-1 - t)).start()
            to_core(7 - t, core).start()
        to_left(t, at(1 + t)).wait_recv()
        if t < 3:
            to_left(t + 1, at(1 + t)).start()
            to_core(1 + t, core).start()
    to_core(4, core).start()
    pltpu.make_async_copy(tile, tile, loc_sem.at[0]).wait()
    load_strip.wait()
    for o in range(NZ):
        to_core(o, 1 - core).wait_recv()

    first_block = col * (COLS // BLK)

    def lower_product(blocks, panel):
        def take(k):
            local = blocks[k] - first_block
            inside = jnp.logical_and(local >= 0, local < COLS // BLK)
            block = tile[jnp.clip(local, 0, COLS // BLK - 1)].reshape(ROWS, BLK)
            pick_l[:, pl.ds(pl.multiple_of(k * BLK, BLK), BLK)] = kept(block, inside)

        each(R, take)

        def multiply(i):
            part = pl.ds(pl.multiple_of(i * 256, BLK), 256)
            prod[panel, :, part] = dot(pick_l[...], unit[panel, :, :, :, :, part].reshape(R * BLK, 256))

        each(2, multiply)

    lower_product(list_below, 0)
    lower_product(blocks_below, 1)

    def onto_rows(blocks, panel, at_slot):
        for i in range(3):
            half = row * 3 + i
            block = lax.div(half, 2)
            offset = lax.rem(half, 2)

            place, found = jnp.int32(0), jnp.int32(0)
            for k in range(R):
                hit = (blocks[k] == block).astype(jnp.int32)
                place, found = place + hit * k, found + hit
            place = jnp.minimum(place, R - 1)
            at_xy, at_z = lax.div(place, 2), lax.rem(place, 2) * 4 + offset * 2
            for j in range(2):
                rows = unit[panel, at_xy, at_z + j].reshape(32, W)
                onto[at_slot, pl.ds(64 * i + 32 * j, 32), :] = kept(rows, found)

    onto_rows(list_beside, 2, 0)
    onto_rows(blocks_beside, 3, 1)

    def finish_lower(i):
        part = pl.ds(pl.multiple_of(i * 64, 64), 64)
        first = -prod[0, part, :]
        second = prod[1, part, :]
        first_b = first.astype(BF16)
        third = -second - dot(first_b, link_b[...])
        prod[0, part, :] = first
        prod[1, part, :] = third
        pick_l[part, 0:W] = first_b
        pick_l[part, W : 2 * W] = second.astype(BF16)
        pick_l[part, 2 * W : 3 * W] = third.astype(BF16)

    each(3, finish_lower)

    def sums(i):
        part = pl.ds(pl.multiple_of(i * BLK, BLK), BLK)
        to = pl.ds(i * 8, 8)
        a = onto[0, :, part]
        sums_s[to, 0] = dot_rows(a, pick_l[:, 0:W]).astype(BF16).reshape(8, 16, W)
        sums_s[to, 1] = dot_rows(a, pick_l[:, W : 2 * W]).astype(BF16).reshape(8, 16, W)
        sums_s[to, 2] = dot_rows(onto[1, :, part], pick_l[:, 2 * W : 3 * W]).astype(BF16).reshape(8, 16, W)

    each(4, sums)
    low_s[...] = prod[:, :, other_half].astype(BF16)
    sums_r[d] = sums_s[d]

    def plane_copy(src, dst, s, r, peer):
        pq = lax.div(peer, 2)
        return copy(src, dst, s, r, row_of(lax.div(pq, NK), z, lax.rem(pq, NK)), lax.rem(peer, 2))

    def sums_out(i):
        peer = lax.rem(d + 1 + i, ND)
        return plane_copy(sums_s.at[peer], sums_r.at[d], sm_s.at[i], sm_r.at[i], peer)

    def sums_in(i):
        peer = lax.rem(d + ND - 1 - i, ND)
        return plane_copy(sums_s.at[d], sums_r.at[peer], sm_s.at[i], sm_r.at[i], peer)

    each(ND - 1, lambda i: sums_out(i).start())
    low_out = copy(low_s, low_r, lw_s.at[0], lw_r.at[0], row, 1 - col)
    low_out.start()

    each(NQ - 1, lambda i: aa_copy(i, lax.rem(q + NQ - 1 - i, NQ), q).wait_recv())

    def upper_product(blocks, panel, slot):
        def take(k):
            b = blocks[k]
            inside = lax.rem(lax.div(b, 3), NZ) == z
            first = lax.div(b, 3 * NZ) * 6 + lax.rem(b, 3) * 2
            pick_u[2 * k] = kept(strip[first], inside)
            pick_u[2 * k + 1] = kept(strip[first + 1], inside)

        each(R, take)

        def multiply(i):
            part = pl.ds(pl.multiple_of(i * BLK, BLK), BLK)
            up_s[slot, part, :] = dot_rows(pick_u[:, :, part].reshape(R * BLK, BLK), unit[panel].reshape(R * BLK, W)).astype(BF16)

        each(STRIP // BLK, multiply)

    upper_product(list_beside, 2, 0)
    upper_product(blocks_beside, 3, 1)

    def up_target(t):
        return row_of(xy, core * 4 + lax.div(t, 2), lax.rem(t, 2))

    def up_rows(t):
        return up_s.at[:, pl.ds(pl.multiple_of(t * OWN, 32), OWN), :]

    def up_out(t):
        return copy(up_rows(t), up_r.at[z], up_ss.at[t], up_rs.at[z], up_target(t), col)

    def up_start(t):
        @pl.when(up_target(t) != row)
        def _():
            up_out(t).start()

    feeder = lax.div(z, 4)
    keeps = core == feeder

    @pl.when(keeps)
    def _():
        t_own = (z - core * 4) * 2 + core
        up_r[z] = up_s[:, pl.ds(pl.multiple_of(t_own * OWN, 32), OWN), :]

    each(4, lambda t: up_start(t))

    each(ND - 1, lambda i: sums_in(i).wait_recv())
    total = jnp.zeros((3, 16, W), F32)
    total = lax.fori_loop(0, ND, lambda i, t: t + sums_r[i].astype(F32), total)
    zsum[z] = total.astype(BF16)

    def z_out(i):
        return copy(zsum.at[z], zsum.at[z], zs_s.at[i], zs_r.at[i], row_of(xy, lax.rem(z + 1 + i, NZ), core), col)

    def z_in(i):
        frm = lax.rem(z + NZ - 1 - i, NZ)
        return copy(zsum.at[frm], zsum.at[frm], zs_s.at[i], zs_r.at[i], row_of(xy, frm, core), col)

    each(NZ - 1, lambda i: z_out(i).start())
    each(4, lambda t: up_start(t + 4))

    copy(low_s, low_r, lw_s.at[0], lw_r.at[0], row, 1 - col).wait_recv()
    o_lower[...] = (prod[0, :, own_half] + low_r[0].astype(F32)).astype(BF16)
    o_nlower[...] = (prod[1, :, own_half] + low_r[1].astype(F32)).astype(BF16)

    each(NZ - 1, lambda i: z_in(i).wait_recv())
    total = jnp.zeros((3, 16, W), F32)
    total = lax.fori_loop(0, NZ, lambda i, t: t + zsum[i].astype(F32), total)
    diag = (base1[...] - total[0]).astype(BF16)
    fin[d, 0] = diag
    fin[d, 1] = (total[1] - dot(diag, link_b[...])).astype(BF16)
    fin[d, 2] = total[2].astype(BF16)

    def fin_out(i):
        peer = lax.rem(d + 1 + i, ND)
        return plane_copy(fin.at[d], fin.at[d], fn_s.at[i], fn_r.at[i], peer)

    def fin_in(i):
        peer = lax.rem(d + ND - 1 - i, ND)
        return plane_copy(fin.at[peer], fin.at[peer], fn_s.at[i], fn_r.at[i], peer)

    each(ND - 1, lambda i: fin_out(i).start())

    def up_wait(i):
        @pl.when(jnp.logical_or(i != z, jnp.logical_not(keeps)))
        def _():
            copy(up_rows(0), up_r.at[i], up_ss.at[0], up_rs.at[i], row_of(xy, i, feeder), col).wait_recv()

    each(NZ, up_wait)

    def up_sum(slot):
        return lax.fori_loop(0, NZ, lambda i, t: t + up_r[i, slot].astype(F32), jnp.zeros((OWN, W), F32))

    upper = (-up_sum(0)).astype(BF16)
    o_upper[...] = upper
    o_nupper[...] = (-(up_sum(1) + dot(upper, link_s[...]))).astype(BF16)

    each(ND - 1, lambda i: fin_in(i).wait_recv())
    o_diag[...] = fin[:, 0, :, own_half].reshape(W, HALF)
    o_link[...] = fin[:, 1].reshape(W, W)
    link_half = fin[:, 1, :, own_half].reshape(W, HALF)

    def last(i):
        part = pl.ds(pl.multiple_of(i * BLK, BLK), BLK)
        held = fin[pl.ds(i * 8, 8), 2, :, own_half].reshape(BLK, HALF).astype(F32)
        o_ndiag[part, :] = (base2[part, :] - held - dot_rows(link_s[:, part], link_half)).astype(BF16)

    each(4, last)

    y_out.wait_send()
    for i in (1, 2, 3):
        x_copy(i, x, x).wait_send()
    each(NQ - 1, lambda i: aa_copy(i, q, lax.rem(q + 1 + i, NQ)).wait_send())
    for t in range(4):
        to_right(t, z).wait_send()
        to_left(t, z).wait_send()
    for o in range(NZ):
        to_core(o, core).wait_send()
    each(ND - 1, lambda i: sums_out(i).wait_send())
    low_out.wait_send()
    each(NZ - 1, lambda i: z_out(i).wait_send())
    each(ND - 1, lambda i: fin_out(i).wait_send())

    def up_sent(t):
        @pl.when(up_target(t) != row)
        def _():
            up_out(t).wait_send()

    each(8, up_sent)


def body(*args):
    vm = pl.BlockSpec(memory_space=pltpu.VMEM)
    sm = pl.BlockSpec(memory_space=pltpu.SMEM)
    (anc, p_below, p_beside, inv_l, inv_u, l_below, l_beside, s_below, s_beside, lk_below, lk_beside,
     sec_l, sec_u, b_below, b_beside) = args
    dma = pltpu.SemaphoreType.DMA
    shapes = [(ROWS, HALF), (OWN, W), (W, HALF), (ROWS, HALF), (OWN, W), (W, W), (W, HALF)]
    return pl.pallas_call(
        kernel,
        out_shape=tuple(jax.ShapeDtypeStruct(s, BF16) for s in shapes),
        in_specs=[pl.BlockSpec(memory_space=pl.ANY)] + [vm] * 10 + [sm] * 4,
        out_specs=tuple([vm] * 7),
        scratch_shapes=[
            pltpu.VMEM((COLS // BLK, 3, 64, BLK), BF16),
            pltpu.VMEM((NQ * 3, 64, STRIP), BF16),
            pltpu.VMEM((4, NXY, NZ, NK, 16, W), BF16),
            pltpu.VMEM((ROWS, R * BLK), BF16),
            pltpu.VMEM((2 * R, 64, STRIP), BF16),
            pltpu.VMEM((2, ROWS, W), BF16),
            pltpu.VMEM((2, ROWS, W), F32),
            pltpu.VMEM((2, ROWS, HALF), BF16),
            pltpu.VMEM((2, ROWS, HALF), BF16),
            pltpu.VMEM((ND, 3, 16, W), BF16),
            pltpu.VMEM((ND, 3, 16, W), BF16),
            pltpu.VMEM((NZ, 3, 16, W), BF16),
            pltpu.VMEM((ND, 3, 16, W), BF16),
            pltpu.VMEM((2, STRIP, W), BF16),
            pltpu.VMEM((NZ, 2, OWN, W), BF16),
            pltpu.VMEM((W, W), BF16),
            pltpu.VMEM((W, W), BF16),
            pltpu.VMEM((16, W), F32),
            pltpu.VMEM((W, HALF), F32),
            dma((2,)),
            dma((1,)), dma((1,)),
            dma((3,)), dma((3,)),
            dma((4,)), dma((4,)), dma((4,)), dma((4,)),
            dma((NZ,)), dma((NZ,)),
            dma((NQ - 1,)), dma((NQ - 1,)),
            dma((1,)), dma((1,)),
            dma((ND - 1,)), dma((ND - 1,)),
            dma((NZ - 1,)), dma((NZ - 1,)),
            dma((ND - 1,)), dma((ND - 1,)),
            dma((8,)), dma((NZ,)),
        ],
        compiler_params=pltpu.CompilerParams(
            collective_id=0, has_side_effects=True, vmem_limit_bytes=60 * 1024 * 1024
        ),
    )(anc.reshape(3, 64, COLS), p_below, p_beside, inv_l, inv_u, s_below, s_beside, lk_below, lk_beside, sec_l, sec_u,
      l_below, l_beside, b_below, b_beside)


def solution(mesh):
    panel = P("rows", None)
    return jax.shard_map(
        body,
        mesh=mesh,
        in_specs=(
            P("rows", "cols"), panel, panel, P(), P(), P(), P(), panel, panel,
            P(), P(), P(), P(), P(), P(),
        ),
        out_specs=(
            P("rows", "cols"),
            P(("cols", "rows"), None),
            P(None, "cols"),
            P("rows", "cols"),
            P(("cols", "rows"), None),
            P(),
            P(None, "cols"),
        ),
        check_vma=False,
    )
```

```python
import jax
import jax.numpy as jnp
from jax import lax
from jax.experimental import pallas as pl
from jax.experimental.pallas import tpu as pltpu
from jax.sharding import PartitionSpec as P

MESH = pl.DeviceIdType.MESH
F32 = jnp.float32
BF16 = jnp.bfloat16
NX, NY, NZ, NK = 4, 2, 8, 2
NXY = NX * NY
NQ = NXY * NK
ND = NQ * 2
BLK = 128
W = 512
HALF = 256
R = 16
ROWS = 192
COLS = 12288
STRIP = COLS // NQ
OWN = 96


def dot(a, b):
    return jnp.dot(a, b, preferred_element_type=F32)


def dot_rows(a, b):
    return lax.dot_general(a, b, (((0,), (0,)), ((), ())), preferred_element_type=F32)


def dot_cols(a, b):
    return lax.dot_general(a, b, (((1,), (1,)), ((), ())), preferred_element_type=F32)


def kept(block, keep):
    scale = jnp.full((1, block.shape[1]), keep.astype(jnp.int32).astype(F32), F32).astype(BF16)
    return block * scale


def each(n, body):
    def step(i, carry):
        body(i)
        return carry

    lax.fori_loop(0, n, step, 0)


def kernel(
    anc, p_below, p_beside, inv_l, inv_u, s_below, s_beside, lk_below, lk_beside, sec_l, sec_u,
    list_below, list_beside, blocks_below, blocks_beside,
    o_lower, o_upper, o_diag, o_nlower, o_nupper, o_link, o_ndiag,
    tile, strip, unit, pick_l, pick_u, onto, prod, low_s, low_r, sums_s, half_r, half_s, sums_r, zsum, fin_s, fin, up_s, up_r,
    link_b, link_s, base1, base2,
    loc_sem, gy_s, gy_r, gx_s, gx_r, zr_s, zr_r, zl_s, zl_r, gc_s, gc_r,
    aa_s, aa_r, lw_s, lw_r, hf_s, hf_r, sm_s, sm_r, zs_s, zs_r, fn_s, fn_r, fc_s, fc_r, up_ss, up_rs,
):
    row = lax.axis_index("rows")
    col = lax.axis_index("cols")
    core = lax.rem(row, NK)
    z = lax.rem(lax.div(row, NK), NZ)
    xy = lax.div(row, NK * NZ)
    x = lax.div(xy, NY)
    yh = lax.rem(xy, NY)
    q = xy * NK + core
    d = q * 2 + col
    e = xy * 2 + col

    def row_of(xy_, z_, core_):
        return (xy_ * NZ + z_) * NK + core_

    def copy(src, dst, s, r, to_row, to_col):
        return pltpu.make_async_remote_copy(
            src_ref=src, dst_ref=dst, send_sem=s, recv_sem=r,
            device_id=(to_row, to_col), device_id_type=MESH,
        )

    def strip_cols(q_):
        return pl.ds(pl.multiple_of(q_ * STRIP, BLK), STRIP)

    own_half = pl.ds(pl.multiple_of(col * HALF, BLK), HALF)
    other_half = pl.ds(pl.multiple_of((1 - col) * HALF, BLK), HALF)

    def load_block(j):
        pltpu.make_async_copy(
            anc.at[:, :, pl.ds(pl.multiple_of(j * BLK, BLK), BLK)], tile.at[j], loc_sem.at[0]
        ).start()

    each(COLS // BLK, load_block)
    load_strip = pltpu.make_async_copy(
        anc.at[:, :, strip_cols(q)], strip.at[pl.ds(q * 3, 3)], loc_sem.at[1]
    )
    load_strip.start()

    unit[0, xy, z, core] = dot(p_below[...], inv_l[...]).astype(BF16)
    unit[1, xy, z, core] = dot(s_below[...], sec_l[...]).astype(BF16)
    unit[2, xy, z, core] = dot_cols(p_beside[...], inv_u[...]).astype(BF16)
    unit[3, xy, z, core] = dot_cols(s_beside[...], sec_u[...]).astype(BF16)

    barrier = pltpu.get_barrier_semaphore()

    def greet_plane(i):
        peer = lax.rem(d + 1 + i, ND)
        pq = lax.div(peer, 2)
        pl.semaphore_signal(
            barrier, inc=1,
            device_id=(row_of(lax.div(pq, NK), z, lax.rem(pq, NK)), lax.rem(peer, 2)),
            device_id_type=MESH,
        )

    def greet(to_row, to_col):
        pl.semaphore_signal(barrier, inc=1, device_id=(to_row, to_col), device_id_type=MESH)

    each(ND - 1, greet_plane)
    each((NZ - 1) * NK, lambda i: greet(row_of(xy, lax.rem(z + 1 + lax.div(i, NK), NZ), lax.rem(i, NK)), col))
    pl.semaphore_wait(barrier, ND - 1 + (NZ - 1) * NK)

    feeder = lax.div(z, 4)

    def up_target(t):
        return row_of(xy, core * 4 + lax.div(t, 2), lax.rem(t, 2))

    nxy = x * NY + (1 - yh)
    mine = unit.at[:, xy, z, core]
    y_out = copy(mine, mine, gy_s.at[0], gy_r.at[0], row_of(nxy, z, core), 1 - col)
    y_out.start()
    theirs = unit.at[:, nxy, z, core]
    copy(theirs, theirs, gy_s.at[0], gy_r.at[0], row_of(nxy, z, core), 1 - col).wait_recv()

    def x_copy(i, holder, to):
        part = unit.at[:, pl.ds(holder * NY, NY), z, core]
        return copy(part, part, gx_s.at[i - 1], gx_r.at[i - 1], row_of(to * NY + yh, z, core), col)

    for i in (1, 3, 2):
        x_copy(i, x, lax.rem(x + i, NX)).start()

    def aa_peer(i, sign):
        j, a = divmod(i, 4)
        step = (1, 3, 2, 0)[a]
        px = lax.rem(x + NX + sign * step, NX)
        py = lax.rem(yh + (j + a) % 2, NY)
        pk = lax.rem(core + j // 2, NK)
        return (px * NY + py) * NK + pk

    def aa_copy(i, src_q, to_q):
        return copy(
            anc.at[:, :, strip_cols(to_q)],
            strip.at[pl.ds(src_q * 3, 3)],
            aa_s.at[i], aa_r.at[i],
            row_of(lax.div(to_q, NK), z, lax.rem(to_q, NK)), col,
        )

    aa_all = [i for i in range(NQ) if ((1, 3, 2, 0)[i % 4], (i // 4 + i % 4) % 2, i // 8) != (0, 0, 0)]

    def aa_out(i):
        return aa_copy(i, q, aa_peer(i, 1))

    def aa_in(i):
        return aa_copy(i, aa_peer(i, -1), q)

    def aa_group(j):
        for i in aa_all:
            if i // 4 == j:
                aa_out(i).start()

    aa_group(0)

    for i in (1, 3, 2):
        frm = lax.rem(x + NX - i, NX)
        x_copy(i, frm, frm).wait_recv()

    right, left = lax.rem(z + 1, NZ), lax.rem(z + NZ - 1, NZ)

    def chunk(zz, lo, n):
        return unit.at[pl.ds(lo, n), :, zz, core]

    def to_right(t, zz):
        part = chunk(zz, 0, 4 if t < 3 else 2)
        return copy(part, part, zr_s.at[t], zr_r.at[t], row_of(xy, right, core), col)

    def to_left(t, zz):
        part = chunk(zz, 0 if t < 3 else 2, 4 if t < 3 else 2)
        return copy(part, part, zl_s.at[t], zl_r.at[t], row_of(xy, left, core), col)

    def to_core(o, k):
        part = unit.at[:, :, lax.rem(z + o, NZ), k]
        return copy(part, part, gc_s.at[o], gc_r.at[o], row_of(xy, z, 1 - core), col)

    def at(o):
        return lax.rem(z + NZ + o, NZ)

    to_right(0, z).start()
    to_left(0, z).start()
    to_core(0, core).start()

    def small(i):
        part = pl.ds(pl.multiple_of(i * BLK, BLK), BLK)
        link_b[part, :] = dot(lk_below[part, :], sec_l[...]).astype(BF16)
        link_s[part, :] = dot_cols(lk_beside[part, :], sec_u[...]).astype(BF16)
        base2[part, :] = dot(sec_u[part, :], sec_l[:, own_half])

    each(4, small)
    base1[...] = dot(inv_u[pl.ds(pl.multiple_of(d * 16, 16), 16), :], inv_l[...])

    for t in range(4):
        to_right(t, at(-1 - t)).wait_recv()
        if t < 3:
            to_right(t + 1, at(-1 - t)).start()
            to_core(7 - t, core).start()
        to_left(t, at(1 + t)).wait_recv()
        if t < 3:
            to_left(t + 1, at(1 + t)).start()
            to_core(1 + t, core).start()
            aa_group(t + 1)
    to_core(4, core).start()
    pltpu.make_async_copy(tile, tile, loc_sem.at[0]).wait()
    load_strip.wait()
    for o in range(NZ):
        to_core(o, 1 - core).wait_recv()

    first_block = col * (COLS // BLK)

    def lower_product(blocks, panel):
        def take(k):
            local = blocks[k] - first_block
            inside = jnp.logical_and(local >= 0, local < COLS // BLK)
            block = tile[jnp.clip(local, 0, COLS // BLK - 1)].reshape(ROWS, BLK)
            pick_l[:, pl.ds(pl.multiple_of(k * BLK, BLK), BLK)] = kept(block, inside)

        each(R, take)

        def multiply(i):
            part = pl.ds(pl.multiple_of(i * 256, BLK), 256)
            prod[panel, :, part] = dot(pick_l[...], unit[panel, :, :, :, :, part].reshape(R * BLK, 256))

        each(2, multiply)

    lower_product(list_below, 0)
    lower_product(blocks_below, 1)

    def onto_rows(blocks, panel, at_slot):
        for i in range(3):
            half = row * 3 + i
            block = lax.div(half, 2)
            offset = lax.rem(half, 2)

            place, found = jnp.int32(0), jnp.int32(0)
            for k in range(R):
                hit = (blocks[k] == block).astype(jnp.int32)
                place, found = place + hit * k, found + hit
            place = jnp.minimum(place, R - 1)
            at_xy, at_z = lax.div(place, 2), lax.rem(place, 2) * 4 + offset * 2
            for j in range(2):
                rows = unit[panel, at_xy, at_z + j].reshape(32, W)
                onto[at_slot, pl.ds(64 * i + 32 * j, 32), :] = kept(rows, found)

    onto_rows(list_beside, 2, 0)
    onto_rows(blocks_beside, 3, 1)

    def finish_lower(i):
        part = pl.ds(pl.multiple_of(i * 64, 64), 64)
        first = -prod[0, part, :]
        second = prod[1, part, :]
        first_b = first.astype(BF16)
        third = -second - dot(first_b, link_b[...])
        prod[0, part, :] = first
        prod[1, part, :] = third
        pick_l[part, 0:W] = first_b
        pick_l[part, W : 2 * W] = second.astype(BF16)
        pick_l[part, 2 * W : 3 * W] = third.astype(BF16)

    each(3, finish_lower)

    def sums(i):
        part = pl.ds(pl.multiple_of(i * BLK, BLK), BLK)
        to = pl.ds(i * 2, 2)
        a = onto[0, :, part]
        sums_s[to, :, :, 0] = dot_rows(a, pick_l[:, 0:W]).astype(BF16).reshape(2, 2, 2, 16, W)
        sums_s[to, :, :, 1] = dot_rows(a, pick_l[:, W : 2 * W]).astype(BF16).reshape(2, 2, 2, 16, W)
        sums_s[to, :, :, 2] = dot_rows(onto[1, :, part], pick_l[:, 2 * W : 3 * W]).astype(BF16).reshape(2, 2, 2, 16, W)

    each(4, sums)
    low_s[...] = prod[:, :, other_half].astype(BF16)

    half_out = copy(sums_s.at[:, 1 - core], half_r, hf_s.at[0], hf_r.at[0], row_of(xy, z, 1 - core), col)
    half_out.start()
    copy(sums_s.at[:, core], half_r, hf_s.at[0], hf_r.at[0], row_of(xy, z, 1 - core), col).wait_recv()

    def halve(i):
        half_s[i] = (sums_s[i, core].astype(F32) + half_r[i].astype(F32)).astype(BF16)

    each(NXY, halve)
    sums_r[e] = half_s[xy, col]

    y = yh * 2 + col
    steps = [
        (1, 0), (0, 1), (3, 0), (0, 3), (1, 1), (3, 3), (1, 3), (3, 1),
        (2, 0), (0, 2), (2, 1), (1, 2), (2, 3), (3, 2), (2, 2),
    ]

    def mate_at(i, sign):
        px = lax.rem(x + NX + sign * steps[i][0], NX)
        py = lax.rem(y + 4 + sign * steps[i][1], 4)
        return px * 4 + py

    def mate(src, dst, s, r, peer):
        return copy(src, dst, s, r, row_of(lax.div(peer, 2), z, core), lax.rem(peer, 2))

    def sums_out(i):
        peer = mate_at(i, 1)
        return mate(half_s.at[lax.div(peer, 2), lax.rem(peer, 2)], sums_r.at[e], sm_s.at[i], sm_r.at[i], peer)

    def sums_in(i):
        peer = mate_at(i, -1)
        return mate(half_s.at[xy, col], sums_r.at[peer], sm_s.at[i], sm_r.at[i], peer)

    for i in range(NQ - 1):
        sums_out(i).start()
    low_out = copy(low_s, low_r, lw_s.at[0], lw_r.at[0], row, 1 - col)
    low_out.start()

    for i in aa_all:
        aa_in(i).wait_recv()

    def upper_product(blocks, panel, slot):
        def take(k):
            b = blocks[k]
            inside = lax.rem(lax.div(b, 3), NZ) == z
            first = lax.div(b, 3 * NZ) * 6 + lax.rem(b, 3) * 2
            pick_u[2 * k] = kept(strip[first], inside)
            pick_u[2 * k + 1] = kept(strip[first + 1], inside)

        each(R, take)

        def multiply(i):
            part = pl.ds(pl.multiple_of(i * BLK, BLK), BLK)
            up_s[slot, part, :] = dot_rows(pick_u[:, :, part].reshape(R * BLK, BLK), unit[panel].reshape(R * BLK, W)).astype(BF16)

        each(STRIP // BLK, multiply)

    def up_out(slot, t):
        rows = up_s.at[slot, pl.ds(pl.multiple_of(t * OWN, 32), OWN), :]
        return copy(rows, up_r.at[z, slot], up_ss.at[slot, t], up_rs.at[slot, z], up_target(t), col)

    def up_start(slot):
        @pl.when(core == feeder)
        def _():
            t_own = (z - core * 4) * 2 + core
            up_r[z, slot] = up_s[slot, pl.ds(pl.multiple_of(t_own * OWN, 32), OWN), :]

        def start(t):
            @pl.when(up_target(t) != row)
            def _():
                up_out(slot, t).start()

        each(NZ, start)

    upper_product(list_beside, 2, 0)

    for i in range(NQ - 1):
        sums_in(i).wait_recv()
    total = jnp.zeros((3, 16, W), F32)
    total = lax.fori_loop(0, NQ, lambda i, t: t + sums_r[i].astype(F32), total)
    zsum[z] = total.astype(BF16)

    z_steps = (1, 7, 2, 6, 3, 5, 4)

    def z_out(i):
        return copy(zsum.at[z], zsum.at[z], zs_s.at[i], zs_r.at[i], row_of(xy, lax.rem(z + z_steps[i], NZ), core), col)

    def z_in(i):
        frm = lax.rem(z + NZ - z_steps[i], NZ)
        return copy(zsum.at[frm], zsum.at[frm], zs_s.at[i], zs_r.at[i], row_of(xy, frm, core), col)

    for i in range(NZ - 1):
        z_out(i).start()
    up_start(0)
    upper_product(blocks_beside, 3, 1)
    up_start(1)

    copy(low_s, low_r, lw_s.at[0], lw_r.at[0], row, 1 - col).wait_recv()
    o_lower[...] = (prod[0, :, own_half] + low_r[0].astype(F32)).astype(BF16)
    o_nlower[...] = (prod[1, :, own_half] + low_r[1].astype(F32)).astype(BF16)

    for i in range(NZ - 1):
        z_in(i).wait_recv()
    total = jnp.zeros((3, 16, W), F32)
    total = lax.fori_loop(0, NZ, lambda i, t: t + zsum[i].astype(F32), total)
    diag = (base1[...] - total[0]).astype(BF16)
    link = (total[1] - dot(diag, link_b[...])).astype(BF16)
    held = total[2].astype(BF16)
    for c in range(2):
        fin_s[c, :, 0:HALF] = diag[:, c * HALF : (c + 1) * HALF]
        fin_s[c, :, HALF : HALF + W] = link
        fin_s[c, :, HALF + W :] = held[:, c * HALF : (c + 1) * HALF]
    fin[xy, core, col] = fin_s[col]

    def fin_out(i):
        peer = mate_at(i, 1)
        return mate(fin_s.at[lax.rem(peer, 2)], fin.at[xy, core, col], fn_s.at[i], fn_r.at[i], peer)

    def fin_in(i):
        peer = mate_at(i, -1)
        return mate(fin_s.at[col], fin.at[lax.div(peer, 2), core, lax.rem(peer, 2)], fn_s.at[i], fn_r.at[i], peer)

    def fin_core(k):
        return copy(fin.at[:, k], fin.at[:, k], fc_s.at[0], fc_r.at[0], row_of(xy, z, 1 - core), col)

    for i in range(NQ - 1):
        fin_out(i).start()
    for i in range(NQ - 1):
        fin_in(i).wait_recv()
    fin_core(core).start()

    def up_wait(i):
        @pl.when(row_of(xy, i, feeder) != row)
        def _():
            for slot in range(2):
                copy(
                    up_s.at[slot, 0:OWN], up_r.at[i, slot], up_ss.at[slot, 0], up_rs.at[slot, i],
                    row_of(xy, i, feeder), col,
                ).wait_recv()

    each(NZ, up_wait)

    def up_sum(slot):
        return lax.fori_loop(0, NZ, lambda i, t: t + up_r[i, slot].astype(F32), jnp.zeros((OWN, W), F32))

    upper = (-up_sum(0)).astype(BF16)
    o_upper[...] = upper
    o_nupper[...] = (-(up_sum(1) + dot(upper, link_s[...]))).astype(BF16)

    fin_core(1 - core).wait_recv()
    o_diag[...] = fin[:, :, :, :, 0:HALF].reshape(W, HALF)
    o_link[...] = fin[:, :, :, :, HALF : HALF + W].reshape(W, W)
    own_link = pl.ds(pl.multiple_of(HALF + col * HALF, BLK), HALF)
    link_half = fin[:, :, :, :, own_link].reshape(W, HALF)

    def last(i):
        part = pl.ds(pl.multiple_of(i * BLK, BLK), BLK)
        held = fin[pl.ds(i * 2, 2), :, :, :, HALF + W :].reshape(BLK, HALF).astype(F32)
        o_ndiag[part, :] = (base2[part, :] - held - dot_rows(link_s[:, part], link_half)).astype(BF16)

    each(4, last)

    y_out.wait_send()
    for i in (1, 2, 3):
        x_copy(i, x, x).wait_send()
    for i in aa_all:
        aa_out(i).wait_send()
    for t in range(4):
        to_right(t, z).wait_send()
        to_left(t, z).wait_send()
    for o in range(NZ):
        to_core(o, core).wait_send()
    half_out.wait_send()
    for i in range(NQ - 1):
        sums_out(i).wait_send()
        fin_out(i).wait_send()
    low_out.wait_send()
    for i in range(NZ - 1):
        z_out(i).wait_send()
    fin_core(core).wait_send()

    def up_sent(t):
        @pl.when(up_target(t) != row)
        def _():
            up_out(0, t).wait_send()
            up_out(1, t).wait_send()

    each(NZ, up_sent)


def hand_on(*refs):
    for src, dst in zip(refs[:7], refs[7:]):
        dst[...] = src[...]


def body(*args):
    vm = pl.BlockSpec(memory_space=pltpu.VMEM)
    sm = pl.BlockSpec(memory_space=pltpu.SMEM)
    (anc, p_below, p_beside, inv_l, inv_u, l_below, l_beside, s_below, s_beside, lk_below, lk_beside,
     sec_l, sec_u, b_below, b_beside) = args
    dma = pltpu.SemaphoreType.DMA
    shapes = [(ROWS, HALF), (OWN, W), (W, HALF), (ROWS, HALF), (OWN, W), (W, W), (W, HALF)]
    out_shape = tuple(jax.ShapeDtypeStruct(s, BF16) for s in shapes)
    made = pl.pallas_call(
        kernel,
        out_shape=out_shape,
        in_specs=[pl.BlockSpec(memory_space=pl.ANY)] + [vm] * 10 + [sm] * 4,
        out_specs=tuple([vm] * 7),
        scratch_shapes=[
            pltpu.VMEM((COLS // BLK, 3, 64, BLK), BF16),
            pltpu.VMEM((NQ * 3, 64, STRIP), BF16),
            pltpu.VMEM((4, NXY, NZ, NK, 16, W), BF16),
            pltpu.VMEM((ROWS, R * BLK), BF16),
            pltpu.VMEM((2 * R, 64, STRIP), BF16),
            pltpu.VMEM((2, ROWS, W), BF16),
            pltpu.VMEM((2, ROWS, W), F32),
            pltpu.VMEM((2, ROWS, HALF), BF16),
            pltpu.VMEM((2, ROWS, HALF), BF16),
            pltpu.VMEM((NXY, NK, 2, 3, 16, W), BF16),
            pltpu.VMEM((NXY, 2, 3, 16, W), BF16),
            pltpu.VMEM((NXY, 2, 3, 16, W), BF16),
            pltpu.VMEM((NQ, 3, 16, W), BF16),
            pltpu.VMEM((NZ, 3, 16, W), BF16),
            pltpu.VMEM((2, 16, 2 * W), BF16),
            pltpu.VMEM((NXY, NK, 2, 16, 2 * W), BF16),
            pltpu.VMEM((2, STRIP, W), BF16),
            pltpu.VMEM((NZ, 2, OWN, W), BF16),
            pltpu.VMEM((W, W), BF16),
            pltpu.VMEM((W, W), BF16),
            pltpu.VMEM((16, W), F32),
            pltpu.VMEM((W, HALF), F32),
            dma((2,)),
            dma((1,)), dma((1,)),
            dma((3,)), dma((3,)),
            dma((4,)), dma((4,)), dma((4,)), dma((4,)),
            dma((NZ,)), dma((NZ,)),
            dma((NQ,)), dma((NQ,)),
            dma((1,)), dma((1,)),
            dma((1,)), dma((1,)),
            dma((NQ - 1,)), dma((NQ - 1,)),
            dma((NZ - 1,)), dma((NZ - 1,)),
            dma((NQ - 1,)), dma((NQ - 1,)),
            dma((1,)), dma((1,)),
            dma((2, NZ)), dma((2, NZ)),
        ],
        compiler_params=pltpu.CompilerParams(
            collective_id=0, has_side_effects=True, vmem_limit_bytes=60 * 1024 * 1024
        ),
    )(anc.reshape(3, 64, COLS), p_below, p_beside, inv_l, inv_u, s_below, s_beside, lk_below, lk_beside, sec_l, sec_u,
      l_below, l_beside, b_below, b_beside)
    return pl.pallas_call(
        hand_on, out_shape=out_shape, in_specs=[vm] * 7, out_specs=tuple([vm] * 7)
    )(*made)


def solution(mesh):
    panel = P("rows", None)
    return jax.shard_map(
        body,
        mesh=mesh,
        in_specs=(
            P("rows", "cols"), panel, panel, P(), P(), P(), P(), panel, panel,
            P(), P(), P(), P(), P(), P(),
        ),
        out_specs=(
            P("rows", "cols"),
            P(("cols", "rows"), None),
            P(None, "cols"),
            P("rows", "cols"),
            P(("cols", "rows"), None),
            P(),
            P(None, "cols"),
        ),
        check_vma=False,
    )
```
